32 devices in a mesh: shard: 4 (over x, core), ctx: 8 (over z, y).
Axes of the slice: x: 2, y: 2, z: 4, core: 2. Of those that a mesh axis runs over, the one named last changes fastest.
Arguments:
- tokens: bfloat16 [4, 1024, 768], P('shard', 'ctx'), may hold values from -6 to 6
- segments: int32 [4, 1024], P('shard', 'ctx'), may hold values from 0 to 11, never falling along the last dimension, each value on 1 to 640 neighbouring positions
- joint_weight: float32 [768, 2304], P(('shard', 'ctx')), may hold values from -0.21875 to 0.21875
- query_bias: float32 [768], P(('shard', 'ctx')), may hold values from -3 to 3
- value_bias: float32 [768], P(('shard', 'ctx')), may hold values from -1.75 to 1.75
- out_weight: float32 [768, 768], P(('shard', 'ctx')), may hold values from -1.75 to 1.75
- out_bias: float32 [768], P(('shard', 'ctx')), may hold values from -1.75 to 1.75
- mid_gain: float32 [768], P(('shard', 'ctx')), may hold values from 0.1 to 1.9
- mid_shift: float32 [768], P(('shard', 'ctx')), may hold values from -3 to 3
- up_weight: float32 [768, 3072], P(('shard', 'ctx')), may hold values from -0.21875 to 0.21875
- up_bias: float32 [3072], P(('shard', 'ctx')), may hold values from -3 to 3
- down_weight: float32 [3072, 768], P(('shard', 'ctx')), may hold values from -0.109375 to 0.109375
- down_bias: float32 [768], P(('shard', 'ctx')), may hold values from -3 to 3
- final_gain: float32 [768], P(('shard', 'ctx')), may hold values from 0.1 to 1.9
- final_shift: float32 [768], P(('shard', 'ctx')), may hold values from -3 to 3
- cotangent: bfloat16 [4, 1024, 768], P('shard', 'ctx'), may hold values from -6 to 6
Outputs:
- layer_output: bfloat16 [4, 1024, 768], P('shard', 'ctx')
- input_grad: bfloat16 [4, 1024, 768], P('shard', 'ctx')
- grad_joint_weight: float32 [768, 2304], P(('shard', 'ctx'))
- grad_query_bias: float32 [768], P(('shard', 'ctx'))
- grad_value_bias: float32 [768], P(('shard', 'ctx'))
- grad_out_weight: float32 [768, 768], P(('shard', 'ctx'))
- grad_out_bias: float32 [768], P(('shard', 'ctx'))
- grad_mid_gain: float32 [768], P(('shard', 'ctx'))
- grad_mid_shift: float32 [768], P(('shard', 'ctx'))
- grad_up_weight: float32 [768, 3072], P(('shard', 'ctx'))
- grad_up_bias: float32 [3072], P(('shard', 'ctx'))
- grad_down_weight: float32 [3072, 768], P(('shard', 'ctx'))
- grad_down_bias: float32 [768], P(('shard', 'ctx'))
- grad_final_gain: float32 [768], P(('shard', 'ctx'))
- grad_final_shift: float32 [768], P(('shard', 'ctx'))
The draws below stay inside these ranges and needn't reach their ends.
Inputs may be any that keep to these rules, and one draw needn't show every extreme that they name: `segments`: along each sequence the ids never fall; there are 12 documents of 1 to 640 positions, and one of exactly 640 in every sequence.
All inputs are finite; a program needn't handle non-finite values.
Results may differ from the reference program's by a relative error of at most 0.024.
Values may be sent and summed in bfloat16 or wider, within the bound.
No kernel may reach another device: no remote copies, remote signals or barrier semaphores. Data moves between devices by JAX's collectives and lax.ppermute only.
A program may use at most 192 MiB of HBM per device.

```python
import math
import jax
import jax.numpy as jnp
import numpy as np
from jax import lax

D = 768
HEADS = 12
HEAD_DIM = 64
FF = 3072
DOCS = 12
LENGTH = 1024
SEQUENCES = 4
DOC_MOST = 640


def with_spikes(entries, own_key, source, target, parts, factor):
    def block_of(dim):
        return (jnp.arange(entries.shape[dim]) // (entries.shape[dim] // parts)).reshape((-1,) + (1,) * (entries.ndim - 1 - dim))

    one_side = jax.random.permutation(own_key, parts)[block_of(target)]
    far = (block_of(target) + parts // 2) % parts
    return jnp.where((block_of(source) == one_side) | (block_of(source) == far), factor * entries, entries)


def block_levels(own_key, dims, shards, low, top_value):
    level, own = 1.0, jax.random.fold_in(own_key, 6)
    for axis_at, parts in shards:
        steps = jnp.exp(jax.random.uniform(jax.random.fold_in(own, axis_at), (parts,), jnp.float32, low / len(shards), top_value / len(shards)))
        level = level * jnp.repeat(steps, dims[axis_at] // parts).reshape([-1 if axis == axis_at else 1 for axis in range(len(dims))])
    return level


def profile(number_of, total, reach, skew):
    loads = [(1 << 20) // math.isqrt(rank ** skew) + 1 for rank in range(2, number_of + 1)]
    surplus, counts = total - reach - (number_of - 1), [1] * (number_of - 1)
    while surplus > 0:
        movable = [i for i in range(number_of - 1) if counts[i] < reach]
        whole, left = sum([loads[i] for i in movable]), surplus
        for i in movable:
            addition = min(reach - counts[i], max(1, left * loads[i] // whole), surplus)
            counts[i] = counts[i] + addition
            surplus = surplus - addition
    return np.array([reach] + counts)


def ragged_sizes(key, count, total, limit, skew):
    if count == 2:
        one = jax.random.randint(key, (), max(1, total - limit), min(limit, total - 1) + 1)
        return jnp.stack([one, total - one])
    tallies = jnp.asarray(profile(count, total, limit, skew), jnp.int32)
    pairs = (count - 1) // 2
    source_of, sink = tallies[1:1 + 2 * pairs:2], tallies[2:2 + 2 * pairs:2]
    margin = jnp.minimum(source_of - 1, limit - sink)
    passed = jax.random.randint(jax.random.fold_in(key, 1), (pairs,), 0, 1 << 20) % (margin + 1)
    tallies = tallies.at[1:1 + 2 * pairs:2].set(source_of - passed).at[2:2 + 2 * pairs:2].set(sink + passed)
    return tallies[jax.random.permutation(jax.random.fold_in(key, 2), count)]


def gaussian(key, extent, scale, bound, shards=(), held_as=jnp.bfloat16):
    entries = scale * jax.random.normal(key, extent, jnp.float32)
    if shards:
        entries = entries * block_levels(key, extent, shards, -0.22, 0.18)
    return jnp.clip(entries, -bound, bound).astype(held_as)


def gaussian_with(rng, dims, width, bound, pieces, heavy, kind=jnp.bfloat16):
    drawn = width * jax.random.normal(rng, dims, jnp.float32)
    if pieces:
        drawn = drawn * block_levels(rng, dims, pieces, -0.22, 0.18)
    return jnp.clip(with_spikes(drawn, jax.random.fold_in(rng, 3), *heavy), -bound, bound).astype(kind)


def setup_inputs(seed: int = 0) -> dict:
    arg_keys = jax.random.split(jax.random.key(seed), 17)
    tokens = gaussian_with(arg_keys[0], (SEQUENCES, LENGTH, D), 1.0, 6.0, ((0, 4), (1, 8)), (1, 2, 8, 2.0))
    segments = jax.vmap(lambda own: jnp.searchsorted(jnp.cumsum(ragged_sizes(own, DOCS, LENGTH, DOC_MOST, 1)), jnp.arange(LENGTH), side="right"))(jax.random.split(arg_keys[1], SEQUENCES)).reshape((SEQUENCES, LENGTH)).astype(jnp.int32)
    joint_weight = gaussian(arg_keys[2], (D, 3 * D), D ** -0.5, 0.21875, ((0, 32),), jnp.float32)
    query_bias = gaussian(arg_keys[3], (D,), 0.5, 3.0, ((0, 32),), jnp.float32)
    value_bias = gaussian(arg_keys[4], (D,), 0.3, 1.75, ((0, 32),), jnp.float32)
    out_weight = gaussian(arg_keys[5], (D, D), (D // 64) ** -0.5, 1.75, ((0, 32),), jnp.float32)
    out_bias = gaussian(arg_keys[6], (D,), 0.3, 1.75, ((0, 32),), jnp.float32)
    mid_gain = jnp.clip(1.0 + 0.18 * jax.random.normal(arg_keys[7], (D,), jnp.float32), 0.1, 1.9)
    mid_shift = gaussian(arg_keys[8], (D,), 0.5, 3.0, ((0, 32),), jnp.float32)
    up_weight = gaussian(arg_keys[9], (D, FF), D ** -0.5, 0.21875, ((0, 32),), jnp.float32)
    up_bias = gaussian(arg_keys[10], (FF,), 0.5, 3.0, ((0, 32),), jnp.float32)
    down_weight = gaussian(arg_keys[11], (FF, D), FF ** -0.5, 0.109375, ((0, 32),), jnp.float32)
    down_bias = gaussian(arg_keys[12], (D,), 0.5, 3.0, ((0, 32),), jnp.float32)
    final_gain = jnp.clip(1.0 + 0.18 * jax.random.normal(arg_keys[13], (D,), jnp.float32), 0.1, 1.9)
    final_shift = gaussian(arg_keys[14], (D,), 0.5, 3.0, ((0, 32),), jnp.float32)
    cotangent = gaussian(arg_keys[15], (SEQUENCES, LENGTH, D), 1.0, 6.0, ((0, 4), (1, 8)))
    return dict(tokens=tokens, segments=segments, joint_weight=joint_weight, query_bias=query_bias, value_bias=value_bias, out_weight=out_weight, out_bias=out_bias, mid_gain=mid_gain, mid_shift=mid_shift, up_weight=up_weight, up_bias=up_bias, down_weight=down_weight, down_bias=down_bias, final_gain=final_gain, final_shift=final_shift, cotangent=cotangent)


@jax.custom_vjp
def low(v):
    return lax.optimization_barrier(v.astype(jnp.bfloat16)).astype(jnp.float32)

@jax.custom_vjp
def low_back(v):
    return v

def low_keep(v):
    return (low(v), None)

def low_pass(kept, grad):
    return (grad,)

def back_keep(v):
    return (v, None)

def back_low(kept, grad):
    return (low(grad),)
low.defvjp(low_keep, low_pass)
low_back.defvjp(back_keep, back_low)
HIGHEST = lax.Precision.HIGHEST

def normalize(hidden, gain, shift):
    mean_value = lax.optimization_barrier(jnp.mean(hidden, axis=-1, keepdims=True))
    centered = hidden - mean_value
    variance = lax.optimization_barrier(jnp.mean(centered * centered, axis=-1, keepdims=True))
    return centered * lax.rsqrt(variance + 1e-05) * gain + shift

def one_sequence(inputs, params):
    hidden_in, docs = inputs
    joint_w, query_b, value_b, out_w, out_b, mid_g, mid_s, up_w, up_b, down_w, down_b, final_g, final_s = params
    joint_shift = jnp.concatenate([query_b, jnp.zeros_like(query_b), value_b])
    projected = jnp.dot(hidden_in, joint_w, precision=HIGHEST) + joint_shift
    projected = low_back(low(projected))
    query = projected[:, :D].reshape(LENGTH, HEADS, HEAD_DIM)
    keys = projected[:, D:2 * D].reshape(LENGTH, HEADS, HEAD_DIM)
    values = projected[:, 2 * D:].reshape(LENGTH, HEADS, HEAD_DIM)
    block_len = math.gcd(LENGTH, 512)
    block_count = LENGTH // block_len
    scale_factor = HEAD_DIM ** (-0.5)

    def attend(block_inputs):
        query_block, docs_block = block_inputs
        logits = jnp.einsum('qhe,khe->hqk', query_block, keys, precision=HIGHEST) * scale_factor
        logits = low_back(logits)
        same_doc = docs_block[:, None] == docs[None, :]
        logits = jnp.where(same_doc[None, :, :], logits, -1e+30)
        probs = low(jax.nn.softmax(logits, axis=-1))
        return jnp.einsum('hqk,khe->qhe', probs, values, precision=HIGHEST)
    mixed = lax.map(jax.checkpoint(attend), (query.reshape(block_count, block_len, HEADS, HEAD_DIM), docs.reshape(block_count, block_len)))
    mixed = low_back(low(mixed.reshape(LENGTH, D)))
    attn_branch = low_back(jnp.dot(mixed, out_w, precision=HIGHEST) + out_b)
    mid = normalize(hidden_in + attn_branch, mid_g, mid_s)
    up_value = low_back(jnp.dot(low(mid), up_w, precision=HIGHEST) + up_b)
    activated = low(jax.nn.gelu(up_value, approximate=False))
    ffn_branch = low_back(jnp.dot(activated, down_w, precision=HIGHEST) + down_b)
    return normalize(mid + ffn_branch, final_g, final_s)

def reference(tokens, segments, joint_weight, query_bias, value_bias, out_weight, out_bias, mid_gain, mid_shift, up_weight, up_bias, down_weight, down_bias, final_gain, final_shift, cotangent):
    params = (joint_weight, query_bias, value_bias, out_weight, out_bias, mid_gain, mid_shift, up_weight, up_bias, down_weight, down_bias, final_gain, final_shift)

    def forward(hidden_all, param_list):
        lowered = tuple((low(item) for item in param_list))

        def run_one(inputs):
            return one_sequence(inputs, lowered)
        return lax.map(jax.checkpoint(run_one), (hidden_all, segments))
    hidden_all = tokens.astype(jnp.float32)
    output, pullback = jax.vjp(forward, hidden_all, params)
    grad_hidden, grads = pullback(cotangent.astype(jnp.float32))
    return (output.astype(jnp.bfloat16), grad_hidden.astype(jnp.bfloat16), grads[0], grads[1], grads[2], grads[3], grads[4], grads[5], grads[6], grads[7], grads[8], grads[9], grads[10], grads[11], grads[12])
```

```python
import functools

import jax
import jax.numpy as jnp
from jax import lax
from jax.experimental import pallas as pl
from jax.experimental.pallas import tpu as pltpu
from jax.sharding import PartitionSpec as P

HEADS = 12
MASKED = -1e30
EPSILON = 1e-05
BF = jnp.bfloat16
F32 = jnp.float32
EXTRA = 64
PAD = 16
AXES = ("shard", "ctx")


def dot(a, b, dims=((1,), (0,))):
    return lax.dot_general(a, b, (dims, ((), ())), preferred_element_type=F32)


def normalize_fwd(hidden, gain, shift):
    center = hidden - jnp.mean(hidden, axis=-1, keepdims=True)
    inverse_dev = lax.rsqrt(jnp.mean(center * center, axis=-1, keepdims=True) + EPSILON)
    normed = center * inverse_dev
    return normed * gain + shift, normed, inverse_dev


def normalize_back(upstream, normed, inverse_dev, gain):
    scaled = upstream * gain
    inner = (
        scaled
        - jnp.mean(scaled, axis=-1, keepdims=True)
        - normed * jnp.mean(scaled * normed, axis=-1, keepdims=True)
    )
    return inner * inverse_dev, jnp.sum(upstream * normed, axis=0), jnp.sum(upstream, axis=0)


def key_chunk(total):
    return total if total <= 1024 else 1024


def attn_fwd_kernel(heads, dim, block, q_ref, kv_ref, segq_ref, segk_ref, o_ref, lse_ref, segb):
    total = kv_ref.shape[0]
    width = heads * dim
    chunk = key_chunk(total)
    steps = total // chunk
    segb[...] = jnp.broadcast_to(segk_ref[...], segb.shape)
    scale = dim ** (-0.5)

    def scores(h, n, qh, begin):
        kh = kv_ref[pl.ds(begin, chunk), h * dim : (h + 1) * dim]
        s = dot(kh, qh, ((1,), (1,)))
        same = segb[pl.ds(begin, chunk), :] == segq_ref[n]
        return jnp.where(same, s, MASKED)

    for h in range(heads):
        vcols = slice(width + h * dim, width + (h + 1) * dim)

        def query_step(n, _, h=h, vcols=vcols):
            rows = pl.ds(pl.multiple_of(n * block, block), block)
            qh = q_ref[rows, h * dim : (h + 1) * dim] * jnp.asarray(scale, BF)
            if steps == 1:
                s = scores(h, n, qh, 0)
                m = jnp.max(s, axis=0, keepdims=True)
                p = jnp.exp(s - m)
                l = jnp.sum(p, axis=0, keepdims=True)
                acc = dot(kv_ref[:, vcols], p.astype(BF), ((0,), (0,)))
            else:

                def chunk_step(i, carry):
                    m0, l0, acc0 = carry
                    begin = pl.multiple_of(i * chunk, chunk)
                    s = scores(h, n, qh, begin)
                    m1 = jnp.maximum(m0, jnp.max(s, axis=0, keepdims=True))
                    p = jnp.exp(s - m1)
                    f = jnp.exp(m0 - m1)
                    l1 = l0 * f + jnp.sum(p, axis=0, keepdims=True)
                    part = dot(kv_ref[pl.ds(begin, chunk), vcols], p.astype(BF), ((0,), (0,)))
                    return m1, l1, acc0 * f + part

                start = (
                    jnp.full((1, block), MASKED, F32),
                    jnp.zeros((1, block), F32),
                    jnp.zeros((dim, block), F32),
                )
                m, l, acc = lax.fori_loop(0, steps, chunk_step, start)
            o_ref[rows, h * dim : (h + 1) * dim] = jnp.transpose(acc / l).astype(BF)
            lse_ref[h, n] = m + jnp.log(l)
            return 0

        lax.fori_loop(0, q_ref.shape[0] // block, query_step, 0)


def attn_bwd_kernel(
    heads, dim, block, q_ref, kv_ref, segq_ref, segk_ref, lse_ref, o_ref, gm_ref, dq_ref, dkv_ref,
    segb, dk_acc, dv_acc,
):
    total = kv_ref.shape[0]
    width = heads * dim
    chunk = key_chunk(total)
    steps = total // chunk
    segb[...] = jnp.broadcast_to(segk_ref[...], segb.shape)
    scale = dim ** (-0.5)
    for h in range(heads):
        cols = slice(h * dim, (h + 1) * dim)
        vcols = slice(width + h * dim, width + (h + 1) * dim)
        dk_acc[...] = jnp.zeros_like(dk_acc)
        dv_acc[...] = jnp.zeros_like(dv_acc)

        def query_step(n, _, h=h, cols=cols, vcols=vcols):
            rows = pl.ds(pl.multiple_of(n * block, block), block)
            qh = q_ref[rows, cols] * jnp.asarray(scale, BF)
            gm = gm_ref[rows, cols]
            prod = gm.astype(F32) * o_ref[rows, cols].astype(F32)
            delta = jnp.sum(jnp.transpose(prod), axis=0, keepdims=True)
            lse = lse_ref[h, n]
            segq = segq_ref[n]

            def part(begin):
                ks = pl.ds(begin, chunk)
                kh = kv_ref[ks, cols]
                s = dot(kh, qh, ((1,), (1,)))
                s = jnp.where(segb[ks, :] == segq, s, MASKED)
                p = jnp.exp(s - lse)
                dp = dot(kv_ref[ks, vcols], gm, ((1,), (1,)))
                ds = (p * (dp - delta)).astype(BF)
                dk_acc[ks, :] += dot(ds, qh)
                dv_acc[ks, :] += dot(p.astype(BF), gm)
                return dot(kh, ds, ((0,), (0,)))

            if steps == 1:
                dqt = part(0)
            else:
                dqt = lax.fori_loop(
                    0,
                    steps,
                    lambda i, acc: acc + part(pl.multiple_of(i * chunk, chunk)),
                    jnp.zeros((dim, block), F32),
                )
            dq_ref[rows, cols] = (jnp.transpose(dqt) * scale).astype(BF)
            return 0

        lax.fori_loop(0, q_ref.shape[0] // block, query_step, 0)
        dkv_ref[:, cols] = dk_acc[...].astype(BF)
        dkv_ref[:, vcols] = dv_acc[...].astype(BF)


def attend(q, kv, segq, segk, heads, dim, block):
    total, rows = kv.shape[0], q.shape[0]
    return pl.pallas_call(
        functools.partial(attn_fwd_kernel, heads, dim, block),
        out_shape=(
            jax.ShapeDtypeStruct((rows, heads * dim), BF),
            jax.ShapeDtypeStruct((heads, rows // block, 1, block), F32),
        ),
        scratch_shapes=[pltpu.VMEM((total, block), F32)],
        name="attend",
    )(q, kv, segq, segk)


def attend_back(q, kv, segq, segk, lse, mixed, gm, heads, dim, block):
    total, rows = kv.shape[0], q.shape[0]
    return pl.pallas_call(
        functools.partial(attn_bwd_kernel, heads, dim, block),
        out_shape=(
            jax.ShapeDtypeStruct((rows, heads * dim), BF),
            jax.ShapeDtypeStruct((total, 2 * heads * dim), BF),
        ),
        scratch_shapes=[
            pltpu.VMEM((total, block), F32),
            pltpu.VMEM((total, dim), F32),
            pltpu.VMEM((total, dim), F32),
        ],
        name="attend_back",
    )(q, kv, segq, segk, lse, mixed, gm)


def place_kernel(count, index_ref, *refs):
    out_ref = refs[count]
    own = index_ref[0]
    for r in range(count):
        out_ref[own ^ r] = refs[r][...]


def place(blocks, index):
    count = len(blocks)
    spec = pl.BlockSpec(memory_space=pltpu.VMEM)
    return pl.pallas_call(
        functools.partial(place_kernel, count),
        out_shape=jax.ShapeDtypeStruct((count,) + blocks[0].shape, blocks[0].dtype),
        in_specs=[pl.BlockSpec(memory_space=pltpu.SMEM)] + [spec] * count,
        out_specs=spec,
        name="place",
    )(index.reshape(1).astype(jnp.int32), *blocks)


def unplace_kernel(count, index_ref, in_ref, *out_refs):
    own = index_ref[0]
    for r in range(count):
        out_refs[r][...] = in_ref[own ^ r]


def unplace(stacked, index):
    count = stacked.shape[0]
    spec = pl.BlockSpec(memory_space=pltpu.VMEM)
    return pl.pallas_call(
        functools.partial(unplace_kernel, count),
        out_shape=[jax.ShapeDtypeStruct(stacked.shape[1:], stacked.dtype)] * count,
        in_specs=[pl.BlockSpec(memory_space=pltpu.SMEM), spec],
        out_specs=[spec] * count,
        name="unplace",
    )(index.reshape(1).astype(jnp.int32), stacked)


def build(shards, ctxs):
    group = ctxs // shards
    custom = group == 2

    def permute(x, where):
        pairs = []
        for s in range(shards):
            for c in range(ctxs):
                s2, a2, b2 = where(s, c // group, c % group)
                pairs.append((s * ctxs + c, s2 * ctxs + a2 * group + b2))
        return lax.ppermute(x, AXES, pairs)

    def swap_plane(x):
        return permute(x, lambda s, a, b: (a, s, b))

    def over_shard(x, k):
        return permute(x, lambda s, a, b: (s ^ k, a, b))

    def over_b(x, j):
        return permute(x, lambda s, a, b: (s, a, b ^ j))

    def over_a(x, i):
        return permute(x, lambda s, a, b: (s, a ^ i, b))

    def gather_shard(x):
        r2 = over_shard(x, 2)
        r1 = over_shard(x, 1)
        r3 = over_shard(r2, 1)
        return [x, r2, r1, r3]

    def scatter_shard(p):
        rows = p.shape[0] // 4
        r = over_shard(p[2 * rows :].astype(BF), 1).astype(F32)
        sent = (p[rows : 2 * rows] + r[rows:]).astype(BF)
        return p[:rows] + r[:rows] + over_shard(sent, 2).astype(F32)

    def gather_ctx(x, index):
        if not custom:
            return lax.all_gather(x, "ctx", axis=0, tiled=False)
        firsts = [x] + [over_a(x, i) for i in range(1, shards)]
        blocks = []
        for f in firsts:
            blocks += [f, over_b(f, 1)]
        return place(blocks, index)

    def scatter_ctx(y, index):
        if not custom:
            return lax.psum_scatter(y, "ctx", scatter_dimension=0, tiled=False).astype(F32)
        rel = unplace(y, index)
        sums = [
            rel[2 * i].astype(F32) + over_b(rel[2 * i + 1], 1).astype(F32) for i in range(shards)
        ]
        total = sums[0]
        for i in range(1, shards):
            total = total + over_a(sums[i].astype(BF), i).astype(F32)
        return total

    def local(
        tokens, segments, joint_weight, query_bias, value_bias, out_weight, out_bias, mid_gain,
        mid_shift, up_weight, up_bias, down_weight, down_bias, final_gain, final_shift, cotangent,
    ):
        _, toks, width = tokens.shape
        rows = joint_weight.shape[0]
        ff_rows = down_weight.shape[0]
        ff_part = up_weight.shape[1] // shards
        per = ff_rows // rows
        heads = HEADS // shards
        dim = width // HEADS
        hw = heads * dim
        own_s = lax.axis_index("shard")
        own_c = lax.axis_index("ctx")

        joint = joint_weight.astype(BF).reshape(rows, 3, shards, hw)
        joint = jnp.transpose(joint, (2, 0, 1, 3)).reshape(shards, rows, 3 * hw)
        small = [query_bias, value_bias, out_bias, mid_gain, mid_shift, down_bias, final_gain, final_shift]
        small = jnp.concatenate(
            [jnp.stack(small, axis=1), up_bias.reshape(rows, per)], axis=1
        ).astype(BF)
        small = jnp.pad(small, ((0, 0), (0, EXTRA - small.shape[1])))
        small = jnp.broadcast_to(small[None], (shards, rows, EXTRA))
        up = jnp.transpose(up_weight.astype(BF).reshape(rows, shards, ff_part), (1, 0, 2))
        payload = jnp.concatenate([joint, small, up], axis=2)
        payload = lax.all_to_all(payload, "shard", 0, 0, tiled=True)
        jw = 3 * hw + EXTRA
        seg_rows = jnp.pad(segments.astype(BF), ((0, PAD - 1), (0, width - toks)))
        mine = swap_plane(jnp.concatenate([tokens[0], seg_rows], axis=0))
        cot = swap_plane(cotangent[0]).astype(F32)
        blocks = []
        for j in range(group):
            blocks += gather_shard(mine if j == 0 else over_b(mine, j))
        table = gather_ctx(payload[:, :, :jw], own_c)
        table = jnp.transpose(table, (1, 0, 2, 3)).reshape(width, jw)
        bulk = jnp.concatenate(
            [
                out_weight.astype(BF),
                down_weight.astype(BF),
                payload[:, :, jw:].reshape(shards * rows, ff_part),
            ],
            axis=0,
        )
        bulk = gather_ctx(bulk, own_c)
        w_out = bulk[:, :rows].reshape(ctxs * rows, width)
        w_down = bulk[:, rows : rows + ff_rows].reshape(ctxs * ff_rows, width)
        w_up = bulk[:, rows + ff_rows :].reshape(ctxs, shards, rows, ff_part)
        w_up = jnp.transpose(w_up, (1, 0, 2, 3)).reshape(width, ff_part)

        w_joint = table[:, : 3 * hw]
        vectors = jnp.transpose(table[:, 3 * hw :].astype(F32))
        out_b, mid_g, mid_s, down_b, final_g, final_s = (vectors[i][None] for i in range(2, 8))
        quarter = lax.dynamic_slice_in_dim(vectors, own_s * hw, hw, 1)
        query_b, value_b = quarter[0], quarter[1]
        up_b = jnp.transpose(
            lax.dynamic_slice_in_dim(vectors, own_s * (width // shards), width // shards, 1)[8 : 8 + per]
        ).reshape(ff_part)
        joint_b = jnp.concatenate([query_b, jnp.zeros((hw,), F32), value_b])

        x_all = jnp.concatenate([b[:toks] for b in blocks], axis=0)
        seg_all = jnp.stack([b[toks, :toks] for b in blocks], axis=0).astype(F32)
        x_own = mine[:toks].astype(F32)
        projected = (dot(x_all, w_joint) + joint_b).astype(BF)
        wide = shards * toks
        q = projected[:wide, :hw]
        kv = projected[:, hw:]
        segq = seg_all[:shards].reshape(shards, 1, toks)
        segk = seg_all.reshape(-1, 1)
        mixed, lse = attend(q, kv, segq, segk, heads, dim, toks)
        attn = scatter_shard(dot(mixed, w_out))
        mid, mid_n, mid_r = normalize_fwd(x_own + attn + out_b, mid_g, mid_s)

        mids = jnp.concatenate(gather_shard(mid.astype(BF)), axis=0)
        up_value = dot(mids, w_up) + up_b
        act, gate_back = jax.vjp(lambda v: jax.nn.gelu(v, approximate=False), up_value)
        act = act.astype(BF)
        ffn = scatter_shard(dot(act, w_down))
        final, final_n, final_r = normalize_fwd(mid + ffn + down_b, final_g, final_s)
        layer_output = swap_plane(final.astype(BF))[None]

        g_y, g_final_gain, g_final_shift = normalize_back(cot, final_n, final_r, final_g)
        g_f = g_y.astype(BF)
        g_down_bias = jnp.sum(g_f.astype(F32), axis=0)
        g_fs = jnp.concatenate(gather_shard(g_f), axis=0)
        g_act = dot(g_fs, w_down, ((1,), (1,)))
        g_u = gate_back(g_act)[0].astype(BF)
        g_mid = g_y + scatter_shard(dot(g_u, w_up, ((1,), (1,))))
        g_down = dot(act, g_fs, ((0,), (0,)))
        g_up = dot(mids, g_u, ((0,), (0,)))
        g_up_bias = jnp.sum(g_u.astype(F32), axis=0)
        g_h, g_mid_gain, g_mid_shift = normalize_back(g_mid, mid_n, mid_r, mid_g)
        g_a = g_h.astype(BF)
        g_out_bias = jnp.sum(g_a.astype(F32), axis=0)
        g_as = jnp.concatenate(gather_shard(g_a), axis=0)
        g_m = dot(g_as, w_out, ((1,), (1,))).astype(BF)
        g_out = dot(mixed, g_as, ((0,), (0,)))

        bulk_grad = jnp.concatenate(
            [
                g_out.astype(BF).reshape(ctxs, rows, width),
                g_down.astype(BF).reshape(ctxs, ff_rows, width),
                jnp.transpose(g_up.astype(BF).reshape(shards, ctxs, rows, ff_part), (1, 0, 2, 3)).reshape(
                    ctxs, shards * rows, ff_part
                ),
            ],
            axis=1,
        )
        bulk_grad = scatter_ctx(bulk_grad, own_c)

        dq, dkv = attend_back(q, kv, segq, segk, lse, mixed, g_m, heads, dim, toks)
        g_joint = jnp.concatenate(
            [dot(x_all[:wide], dq, ((0,), (0,))), dot(x_all, dkv, ((0,), (0,)))], axis=1
        )
        dkv_own = dkv[:wide].astype(F32)
        for j in range(1, group):
            dkv_own = dkv_own + over_b(dkv[j * wide : (j + 1) * wide], j).astype(F32)
        g_qkv = jnp.concatenate([dq, dkv_own.astype(BF)], axis=1)
        g_in = scatter_shard(dot(g_qkv, w_joint, ((1,), (1,))))
        input_grad = swap_plane((g_h + g_in).astype(BF))[None]

        g_query_bias = jnp.sum(dq.astype(F32), axis=0)
        g_value_bias = jnp.sum(dkv[:, hw:].astype(F32), axis=0)

        def spread(v):
            return lax.dynamic_update_slice_in_dim(
                jnp.zeros((width,) + v.shape[1:], F32), v, own_s * v.shape[0], 0
            )

        columns = jnp.stack(
            [
                spread(g_query_bias), spread(g_value_bias), g_out_bias, g_mid_gain, g_mid_shift,
                g_down_bias, g_final_gain, g_final_shift,
            ],
            axis=1,
        )
        columns = jnp.concatenate([columns, spread(g_up_bias.reshape(width // shards, per))], axis=1)
        columns = jnp.pad(columns, ((0, 0), (0, EXTRA - columns.shape[1])))
        g_table = jnp.concatenate([g_joint, columns], axis=1).astype(BF)
        g_table = jnp.transpose(g_table.reshape(shards, ctxs, rows, jw), (1, 0, 2, 3))
        g_table = scatter_ctx(g_table, own_c)
        payload = jnp.concatenate(
            [g_table, bulk_grad[rows + ff_rows :].reshape(shards, rows, ff_part)], axis=2
        ).astype(BF)
        payload = lax.all_to_all(payload, "shard", 0, 0, tiled=True).astype(F32)
        g_joint_weight = jnp.transpose(
            payload[:, :, : 3 * hw].reshape(shards, rows, 3, hw), (1, 2, 0, 3)
        ).reshape(rows, 3 * width)
        g_up_weight = jnp.transpose(payload[:, :, jw:], (1, 0, 2)).reshape(rows, shards * ff_part)
        sums = jnp.sum(payload[:, :, 3 * hw : jw], axis=0)
        return (
            layer_output,
            input_grad,
            g_joint_weight,
            sums[:, 0],
            sums[:, 1],
            bulk_grad[:rows],
            sums[:, 2],
            sums[:, 3],
            sums[:, 4],
            g_up_weight,
            sums[:, 8 : 8 + per].reshape(ff_rows),
            bulk_grad[rows : rows + ff_rows],
            sums[:, 5],
            sums[:, 6],
            sums[:, 7],
        )

    return local


def solution(mesh):
    both = P(AXES)
    mat = P(AXES, None)
    act = P("shard", "ctx", None)
    return jax.shard_map(
        build(mesh.shape["shard"], mesh.shape["ctx"]),
        mesh=mesh,
        in_specs=(
            act, P("shard", "ctx"), mat, both, both, mat, both, both, both, mat, both, mat, both,
            both, both, act,
        ),
        out_specs=(
            act, act, mat, both, both, mat, both, both, both, mat, both, mat, both, both, both,
        ),
        check_vma=False,
    )
```
